1024 devices in a mesh: replica: 64 (over z, y_lo, core), fsdp: 16 (over x, y_hi).
Axes of the slice: x: 8, y: 8 (y_hi: 2, y_lo: 4; y = y_hi * 4 + y_lo), z: 8, core: 2. Of those that a mesh axis runs over, the one named last changes fastest.
Arguments:
- tokens: bfloat16 [131072, 8192], P(('replica', 'fsdp')), may hold values from -6 to 6
- norm_gain: bfloat16 [8192], P('fsdp'), may hold values from 0.099609375 to 1.8984375
- key_weight: bfloat16 [8192, 128], P('fsdp'), may hold values from -0.0625 to 0.0625
- key_cotangent: bfloat16 [131072, 128], P(('replica', 'fsdp')), may hold values from -0.25 to 0.25
- outer_params: float32 [32, 16, 8192], P(None, 'fsdp'), may hold values from -6 to 6
- outer_momentum: float32 [32, 16, 8192], P(None, 'fsdp'), may hold values from -3 to 3
- inner_params: bfloat16 [64, 32, 16, 8192], P('replica', None, 'fsdp'), may hold values from -16 to 16
- fragment: int32 [], replicated, may hold values from 0 to 31
- mix_step: int32 [64], P('replica'), may hold values from 0 to 8
Outputs:
- keys: bfloat16 [131072, 128], P(('replica', 'fsdp'))
- weight_grad: float32 [64, 8192, 128], P('replica', 'fsdp')
- gain_grad: float32 [64, 8192], P('replica', 'fsdp')
- new_outer: float32 [16, 8192], P('fsdp', 'replica')
- new_momentum: float32 [16, 8192], P('fsdp', 'replica')
- new_inner: bfloat16 [64, 16, 8192], P('replica', 'fsdp')
The draws below stay inside these ranges and needn't reach their ends.
All inputs are finite; a program needn't handle non-finite values.
Results may differ from the reference program's by a relative error of at most 0.012.
Values may be sent and summed in bfloat16 or wider, within the bound.
No kernel may reach another device: no remote copies, remote signals or barrier semaphores. Data moves between devices by JAX's collectives and lax.ppermute only.
A program may use at most 32 MiB of HBM per device.

```python
import jax
import jax.numpy as jnp
from jax import lax

D = 8192
HD = 128
TOK_DEV = 128
NFRAG = 32
MIXSTEPS = 8
TOKENS = 131072
FRAG_ROWS = 16
REPLICAS = 64
N_REPLICA = 64
N_FSDP = 16


def touch_ends(array, own_key, low, top_value):
    longest = array.shape.index(max(array.shape))
    spots = []
    for shift in (0, 1):
        where = [jax.random.randint(jax.random.fold_in(own_key, axis), (), 0, length) for axis, length in enumerate(array.shape)]
        where[longest] = (where[longest] + shift) % array.shape[longest]
        spots.append(tuple(where))
    return array.at[spots[0]].set(low).at[spots[1]].set(top_value)


def raised(entries, stream_key, source, target, blocks, factor):
    def block_of(dim):
        return (jnp.arange(entries.shape[dim]) // (entries.shape[dim] // blocks)).reshape((-1,) + (1,) * (entries.ndim - 1 - dim))

    near = jax.random.permutation(stream_key, blocks)[block_of(target)]
    far = (block_of(target) + blocks // 2) % blocks
    return jnp.where((block_of(source) == near) | (block_of(source) == far), factor * entries, entries)


def level_of(own_key, dims, shards, low, largest):
    loudness = 1.0
    for axis_at, blocks in shards:
        heights = jax.random.uniform(jax.random.fold_in(jax.random.fold_in(own_key, 6), axis_at), (blocks,), jnp.float32, low / len(shards), largest / len(shards))
        loudness = loudness * jnp.repeat(jnp.exp(heights), dims[axis_at] // blocks).reshape((-1,) + (1,) * (len(dims) - 1 - axis_at))
    return loudness


def normal_values(key, extent, spread, bound, cuts=(), held_as=jnp.bfloat16):
    result = spread * jax.random.normal(key, extent, jnp.float32)
    if cuts:
        result = result * level_of(key, extent, cuts, -0.22, 0.18)
    return jnp.clip(result, -bound, bound).astype(held_as)


def heavy_noise(stream_key, shape, scale, most, cuts, heavy, dtype=jnp.bfloat16):
    entries = scale * jax.random.normal(stream_key, shape, jnp.float32)
    if cuts:
        entries = entries * level_of(stream_key, shape, cuts, -0.22, 0.18)
    return jnp.clip(raised(entries, jax.random.fold_in(stream_key, 3), *heavy), -most, most).astype(dtype)


def setup_inputs(seed: int = 0) -> dict:
    key_of = jax.random.split(jax.random.key(seed), 10)
    return {
        "tokens": normal_values(key_of[0], (TOKENS, D), 1.0, 6.0, ((0, 1024),)),
        "norm_gain": jnp.clip(1.0 + 0.18 * jax.random.normal(key_of[1], (D,), jnp.float32), 0.099609375, 1.8984375).astype(jnp.bfloat16),
        "key_weight": normal_values(key_of[2], (D, HD), D ** -0.5, 0.0625, ((0, 16),)),
        "key_cotangent": normal_values(key_of[3], (TOKENS, HD), (2.0 * (TOK_DEV * N_FSDP) ** -0.5), 0.25, ((0, 1024),)),
        "outer_params": normal_values(key_of[4], (NFRAG, FRAG_ROWS, D), 1.0, 6.0, ((1, 16),), jnp.float32),
        "outer_momentum": normal_values(key_of[5], (NFRAG, FRAG_ROWS, D), 0.5, 3.0, ((1, 16),), jnp.float32),
        "inner_params": heavy_noise(key_of[6], (REPLICAS, NFRAG, FRAG_ROWS, D), 1.0, 16.0, ((0, 64), (2, 16)), (0, 3, 64, 4.0)),
        "fragment": jax.random.randint(key_of[7], (), 0, NFRAG).astype(jnp.int32),
        "mix_step": touch_ends(jax.random.randint(key_of[8], (REPLICAS,), 0, MIXSTEPS + 1), jax.random.fold_in(key_of[8], 1), 0, MIXSTEPS).astype(jnp.int32),
    }


norm_eps = 1e-05

def reference(tokens, norm_gain, key_weight, key_cotangent, outer_params, outer_momentum, inner_params, fragment, mix_step):
    group_tok = TOK_DEV * N_FSDP
    tok_groups = tokens.reshape(N_REPLICA, group_tok, D)
    cot_groups = key_cotangent.reshape(N_REPLICA, group_tok, HD)
    gain_float = norm_gain.astype(jnp.float32)

    def per_replica(pair):
        tok_rows, cot_rows = pair
        tok_float = tok_rows.astype(jnp.float32)
        inv_rms = lax.rsqrt(lax.optimization_barrier(jnp.mean(tok_float * tok_float, axis=1, keepdims=True)) + norm_eps)
        unit_rows = (tok_float * inv_rms).astype(jnp.bfloat16)
        normed = (unit_rows.astype(jnp.float32) * gain_float).astype(jnp.bfloat16)
        key_out = jnp.dot(normed, key_weight, preferred_element_type=jnp.float32).astype(jnp.bfloat16)
        weight_part = lax.dot_general(normed, cot_rows, (((0,), (0,)), ((), ())), preferred_element_type=jnp.float32)
        grad_normed = lax.dot_general(cot_rows, key_weight, (((1,), (1,)), ((), ())), preferred_element_type=jnp.float32)
        gain_part = lax.optimization_barrier(jnp.sum(grad_normed * unit_rows.astype(jnp.float32), axis=0))
        return (key_out, weight_part, gain_part)
    key_out, weight_grad, gain_grad = lax.map(per_replica, (tok_groups, cot_groups))
    key_out = key_out.reshape(TOKENS, HD)
    index = fragment.astype(jnp.int32)
    outer_now = lax.dynamic_index_in_dim(outer_params, index, 0, keepdims=False)
    momentum_now = lax.dynamic_index_in_dim(outer_momentum, index, 0, keepdims=False)
    inner_now = lax.dynamic_index_in_dim(inner_params, index, 1, keepdims=False).astype(jnp.float32)
    pseudo_grad = lax.optimization_barrier(jnp.sum(outer_now[None] - inner_now, axis=0)) / N_REPLICA
    new_momentum = 0.9 * momentum_now + pseudo_grad
    new_outer = outer_now - 0.7 * (pseudo_grad + 0.9 * new_momentum)
    mix_alpha = ((mix_step.astype(jnp.float32) + 1.0) / (MIXSTEPS + 1.0))[:, None, None]
    new_inner = (mix_alpha * new_outer[None] + (1.0 - mix_alpha) * inner_now).astype(jnp.bfloat16)
    return (key_out, weight_grad, gain_grad, new_outer, new_momentum, new_inner)
```

```python
import jax
import jax.numpy as jnp
from jax import lax
from jax.experimental import pallas as pl
from jax.experimental.pallas import tpu as pltpu
from jax.sharding import PartitionSpec as P

MIXSTEPS = 8
ALL = ("replica", "fsdp")

norm_eps = 1e-05


def route(move):
    pairs = []
    for r in range(64):
        for f in range(16):
            z, y, c, x = r // 8, (r // 2) % 4 + 4 * (f % 2), r % 2, f // 2
            z, y, c, x = move(z, y, c, x)
            pairs.append((r * 16 + f, (z * 8 + y % 4 * 2 + c) * 16 + x * 2 + y // 4))
    return pairs


def permute(value, move):
    return lax.ppermute(value, ALL, route(move))


def other_pair(i, n):
    return (i + 1) % n if i % 2 else (i - 1) % n


def x_near(z, y, c, x):
    return z, y, c, x ^ 1


def x_near_other(z, y, c, x):
    return z, y, c, other_pair(x, 8)


def x_two(z, y, c, x):
    return z, y, c, x ^ 2


def x_two_other(z, y, c, x):
    return z, y, c, other_pair(x // 2, 4) * 2 + x % 2


def x_four(z, y, c, x):
    return z, y, c, x ^ 4


def y_half(z, y, c, x):
    return z, (6, 7, 4, 5, 2, 3, 0, 1)[y], c, x


def core_swap(z, y, c, x):
    return z, y, 1 - c, x


def factor_kernel(tok_ref, cot_ref, inv_ref, keep_a, keep_b, send_a, send_b):
    tokens, width = tok_ref.shape
    hd = cot_ref.shape[1]
    chunk = keep_a.shape[2]
    half = hd // 2

    def squares(i, acc):
        for k in range(chunk // 128):
            t = tok_ref[:, pl.ds(pl.multiple_of(i * chunk + k * 128, 128), 128)].astype(jnp.float32)
            acc = acc + t * t
        return acc

    acc = lax.fori_loop(0, width // chunk, squares, jnp.zeros((tokens, 128), jnp.float32))
    inv = lax.rsqrt(jnp.sum(acc, axis=1, keepdims=True) / width + norm_eps)
    inv_ref[...] = jnp.broadcast_to(inv, inv_ref.shape)
    scaled = (cot_ref[...].astype(jnp.float32) * inv).T.astype(jnp.bfloat16)
    place = lax.axis_index("fsdp")
    x0 = (place // 2) % 2
    x1 = (place // 4) % 2

    def product(b1, b0, rest):
        d1 = x1 + b1 - 2 * b1 * x1
        d0 = x0 + b0 - 2 * b0 * x0
        source = ((rest // 2) * 4 + d1 * 2 + d0) * 2 + rest % 2
        columns = tok_ref[:, pl.ds(pl.multiple_of(source * chunk, chunk), chunk)]
        return jnp.dot(scaled, columns, preferred_element_type=jnp.float32).astype(jnp.bfloat16)

    for b1 in range(2):
        for rest in range(4):
            sent = product(b1, 1, rest)
            send_a[b1 * 4 + rest] = sent[:half]
            send_b[(1 - b1) * 4 + rest] = sent[half:]
            kept = product(b1, 0, rest)
            keep_a[b1 * 4 + rest] = kept[:half]
            keep_b[b1 * 4 + rest] = kept[half:]


def factor_parts(tokens, cot, chunk):
    half = jax.ShapeDtypeStruct((8, cot.shape[1] // 2, chunk), jnp.bfloat16)
    return pl.pallas_call(
        factor_kernel,
        out_shape=(jax.ShapeDtypeStruct((tokens.shape[0], 128), jnp.float32), half, half, half, half),
    )(tokens, cot)


def keys_kernel(tok_ref, inv_ref, near_ref, far_ref, near_core_ref, far_core_ref, out_ref):
    rows = near_ref.shape[1]
    place = lax.axis_index("fsdp")
    core = lax.axis_index("replica") % 2
    acc = jnp.zeros(out_ref.shape, jnp.float32)
    for dc, refs in ((0, (near_ref, far_ref)), (1, (near_core_ref, far_core_ref))):
        for dy, ref in enumerate(refs):
            for slot in range(8):
                dx = (slot // 4) * 1 + (slot // 2 % 2) * 2 + (slot % 2) * 4
                source = place ^ (dx * 2 + dy)
                start = pl.multiple_of((source * 2 + (core ^ dc)) * rows, rows)
                acc = acc + jnp.dot(
                    tok_ref[:, pl.ds(start, rows)], ref[slot], preferred_element_type=jnp.float32
                )
    out_ref[...] = (acc * inv_ref[...]).astype(out_ref.dtype)


def on_device(
    tokens,
    norm_gain,
    key_weight,
    key_cotangent,
    outer_params,
    outer_momentum,
    inner_params,
    fragment,
    mix_step,
):
    rows, hd = key_weight.shape
    gain = norm_gain.astype(jnp.float32)[:, None]
    weight = key_weight.astype(jnp.float32)
    scaled_weight = (gain * weight).astype(jnp.bfloat16)
    replica = lax.axis_index("replica")
    replicas = lax.axis_size("replica")
    shard = lax.dynamic_slice_in_dim(scaled_weight, (replica % 2) * (rows // 2), rows // 2, 0)[None]

    w1 = jnp.concatenate([shard, permute(shard, x_four)])
    inv, keep_a, keep_b, send_a, send_b = factor_parts(tokens, key_cotangent, rows)
    w2 = jnp.concatenate([w1, permute(w1, x_two)])
    recv_a = permute(send_a, x_near)
    recv_b = permute(send_b, x_near_other)

    col_width = outer_params.shape[2] // replicas
    col_start = replica * col_width
    inner_now = lax.dynamic_index_in_dim(inner_params[0], fragment, 0, keepdims=False).astype(
        jnp.float32
    )
    own_outer_now = lax.dynamic_slice(
        outer_params, (fragment, 0, col_start), (1, 1, col_width)
    ).reshape(1, col_width)
    own_momentum_now = lax.dynamic_slice(
        outer_momentum, (fragment, 0, col_start), (1, 1, col_width)
    ).reshape(1, col_width)
    spread = lax.all_to_all(inner_now.reshape(replicas, 1, col_width), "replica", 0, 0)
    pseudo_grad = own_outer_now - jnp.sum(spread, axis=0) / replicas
    own_momentum = 0.9 * own_momentum_now + pseudo_grad
    own_outer = own_outer_now - 0.7 * (pseudo_grad + 0.9 * own_momentum)

    def add(a, b):
        return (a.astype(jnp.float32) + b.astype(jnp.float32)).astype(jnp.bfloat16)

    w3 = jnp.concatenate([w2, permute(w2, x_near)])
    recv2_a = permute(add(keep_a[4:], recv_a[4:]), x_two)
    recv2_b = permute(add(keep_b[4:], recv_b[4:]), x_two_other)
    outer_next = lax.all_to_all(
        jnp.broadcast_to(own_outer[None], (replicas, 1, col_width)), "replica", 0, 0
    ).reshape(1, replicas * col_width)
    mix_alpha = (mix_step[0].astype(jnp.float32) + 1.0) / (MIXSTEPS + 1.0)
    new_inner = (mix_alpha * outer_next + (1.0 - mix_alpha) * inner_now).astype(jnp.bfloat16)

    w_far = permute(w3, y_half)
    w_core = permute(w3, core_swap)
    part_a = add(add(keep_a[:4], recv_a[:4]), recv2_a)
    part_b = add(add(keep_b[:4], recv_b[:4]), recv2_b)
    groups = [[2 * k, 2 * k + 1, 2 * k + 8, 2 * k + 9] for k in range(4)]
    mine = lax.all_to_all(
        jnp.concatenate([part_a, part_b], axis=1), "fsdp", 0, 0, axis_index_groups=groups
    )
    w_far_core = permute(w_far, core_swap)
    factor = jnp.sum(mine.astype(jnp.float32), axis=0).T
    weight_grad = gain * factor
    gain_grad = jnp.sum(weight * factor, axis=1)
    key_out = pl.pallas_call(
        keys_kernel, out_shape=jax.ShapeDtypeStruct((tokens.shape[0], hd), jnp.bfloat16)
    )(tokens, inv, w3, w_far, w_core, w_far_core)
    return (key_out, weight_grad[None], gain_grad[None], own_outer, own_momentum, new_inner[None])


def solution(mesh):
    in_specs = (
        P(("replica", "fsdp"), None),
        P("fsdp"),
        P("fsdp", None),
        P(("replica", "fsdp"), None),
        P(None, "fsdp", None),
        P(None, "fsdp", None),
        P("replica", None, "fsdp", None),
        P(),
        P("replica"),
    )
    out_specs = (
        P(("replica", "fsdp"), None),
        P("replica", "fsdp", None),
        P("replica", "fsdp"),
        P("fsdp", "replica"),
        P("fsdp", "replica"),
        P("replica", "fsdp", None),
    )
    return jax.shard_map(
        on_device, mesh=mesh, in_specs=in_specs, out_specs=out_specs, check_vma=False
    )
```

```python
import jax
import jax.numpy as jnp
from jax import lax
from jax.experimental import pallas as pl
from jax.sharding import PartitionSpec as P


MIXSTEPS = 8
ALL = ("replica", "fsdp")

norm_eps = 1e-05


def route(move):
    pairs = []
    for r in range(64):
        for f in range(16):
            z, y, c, x = r // 8, (r // 2) % 4 + 4 * (f % 2), r % 2, f // 2
            z, y, c, x = move(z, y, c, x)
            pairs.append((r * 16 + f, (z * 8 + y % 4 * 2 + c) * 16 + x * 2 + y // 4))
    return pairs


def permute(value, move):
    return lax.ppermute(value, ALL, route(move))


def other_pair(i, n):
    return (i + 1) % n if i % 2 else (i - 1) % n


def x_near(z, y, c, x):
    return z, y, c, x ^ 1


def x_near_other(z, y, c, x):
    return z, y, c, other_pair(x, 8)


def x_two(z, y, c, x):
    return z, y, c, x ^ 2


def x_four(z, y, c, x):
    return z, y, c, x ^ 4


def y_half(z, y, c, x):
    return z, (6, 7, 4, 5, 2, 3, 0, 1)[y], c, x


def y_one(z, y, c, x):
    return z, y ^ 1, c, x


def y_two(z, y, c, x):
    return z, y ^ 2, c, x


def z_one(z, y, c, x):
    return z ^ 1, y, c, x


def z_two(z, y, c, x):
    return z ^ 2, y, c, x


def z_four(z, y, c, x):
    return z ^ 4, y, c, x


def core_swap(z, y, c, x):
    return z, y, 1 - c, x


def factor_kernel(tok_ref, cot_ref, inv_ref, keep_ref, send_a, send_b):
    tokens, width = tok_ref.shape
    chunk = keep_ref.shape[2]

    def squares(i, acc):
        for k in range(chunk // 128):
            t = tok_ref[:, pl.ds(pl.multiple_of(i * chunk + k * 128, 128), 128)].astype(jnp.float32)
            acc = acc + t * t
        return acc

    acc = lax.fori_loop(0, width // chunk, squares, jnp.zeros((tokens, 128), jnp.float32))
    inv = lax.rsqrt(jnp.sum(acc, axis=1, keepdims=True) / width + norm_eps)
    inv_ref[...] = jnp.broadcast_to(inv, inv_ref.shape)
    scaled = (cot_ref[...].astype(jnp.float32) * inv).T.astype(jnp.bfloat16)
    parity = (lax.axis_index("fsdp") // 2) % 2

    def product(slot, x0):
        source = ((slot // 2) * 2 + x0) * 2 + slot % 2
        columns = tok_ref[:, pl.ds(pl.multiple_of(source * chunk, chunk), chunk)]
        return jnp.dot(scaled, columns, preferred_element_type=jnp.float32).astype(jnp.bfloat16)

    for slot in range(8):
        (send_a, send_b)[slot // 4][slot % 4] = product(slot, 1 - parity)
        keep_ref[slot] = product(slot, parity)


def factor_parts(tokens, cot, chunk):
    hd = cot.shape[1]
    half = jax.ShapeDtypeStruct((4, hd, chunk), jnp.bfloat16)
    return pl.pallas_call(
        factor_kernel,
        out_shape=(
            jax.ShapeDtypeStruct((tokens.shape[0], 128), jnp.float32),
            jax.ShapeDtypeStruct((8, hd, chunk), jnp.bfloat16),
            half,
            half,
        ),
    )(tokens, cot)


def add_kernel(keep_ref, a_ref, b_ref, out_ref):
    for slot in range(8):
        other = (a_ref, b_ref)[slot // 4][slot % 4]
        out_ref[slot] = (keep_ref[slot].astype(jnp.float32) + other.astype(jnp.float32)).astype(
            out_ref.dtype
        )


def add_parts(keep, a, b):
    return pl.pallas_call(
        add_kernel, out_shape=jax.ShapeDtypeStruct(keep.shape, keep.dtype)
    )(keep, a, b)


def keys_product(tok_ref, w_ref, flip):
    shards, rows, hd = w_ref.shape
    core = lax.axis_index("replica") % 2
    half = core + flip - 2 * core * flip
    place = lax.axis_index("fsdp")
    acc = jnp.zeros((tok_ref.shape[0], hd), jnp.float32)
    for slot in range(shards):
        step = (slot // 8) * 2 + (slot // 4 % 2) * 4 + (slot // 2 % 2) + (slot % 2) * 8
        start = pl.multiple_of(((place ^ step) * 2 + half) * rows, rows)
        acc = acc + jnp.dot(
            tok_ref[:, pl.ds(start, rows)], w_ref[slot], preferred_element_type=jnp.float32
        )
    return acc


def keys_first(tok_ref, w_ref, out_ref):
    out_ref[...] = keys_product(tok_ref, w_ref, 0)


def keys_second(tok_ref, w_ref, inv_ref, first_ref, out_ref):
    acc = first_ref[...] + keys_product(tok_ref, w_ref, 1)
    out_ref[...] = (acc * inv_ref[...]).astype(out_ref.dtype)


def step(
    tokens,
    norm_gain,
    key_weight,
    key_cotangent,
    outer_params,
    outer_momentum,
    inner_params,
    fragment,
    mix_step,
):
    rows, hd = key_weight.shape
    replica = lax.axis_index("replica")
    replicas = lax.axis_size("replica")
    core = replica % 2

    inv, keep, send_a, send_b = factor_parts(tokens, key_cotangent, rows)
    recv_a = permute(send_a, x_near)
    recv_b = permute(send_b, x_near_other)

    half = rows // 2
    gain_half = lax.dynamic_slice_in_dim(norm_gain, core * half, half, 0).astype(jnp.float32)
    weight_half = lax.dynamic_slice_in_dim(key_weight, core * half, half, 0).astype(jnp.float32)
    w_half = (gain_half[:, None] * weight_half).astype(jnp.bfloat16)[None]

    def doubled(values, move):
        return jnp.concatenate([values, permute(values, move)])

    w_half = doubled(w_half, x_four)
    w_half = doubled(w_half, y_half)
    part = add_parts(keep, recv_a, recv_b)
    x_groups = [[4 * k + 2 * p + y for k in range(4) for y in range(2)] for p in range(2)]
    mine = lax.all_to_all(part, "fsdp", 0, 0, axis_index_groups=x_groups)
    w_half = doubled(w_half, x_two)
    w_half = doubled(w_half, x_near)

    blocks = (replicas // 2, 2, outer_params.shape[2] // replicas)

    def row_of(values):
        return lax.dynamic_index_in_dim(values, fragment, 0, keepdims=False).reshape(blocks)

    def half_of(values):
        return lax.dynamic_index_in_dim(values, core, 1, keepdims=False)

    inner_row = row_of(inner_params[0])
    other_core = permute(
        lax.dynamic_index_in_dim(inner_row, 1 - core, 1, keepdims=False), core_swap
    )
    total = half_of(inner_row).astype(jnp.float32) + other_core.astype(jnp.float32)
    for move in (y_one, y_two, z_one, z_two, z_four):
        total = total + permute(total, move)
    outer_now = half_of(row_of(outer_params))
    momentum_now = half_of(row_of(outer_momentum))
    pseudo_grad = outer_now - total / replicas
    momentum_next = 0.9 * momentum_now + pseudo_grad
    outer_next = outer_now - 0.7 * (pseudo_grad + 0.9 * momentum_next)
    own_outer = lax.dynamic_slice_in_dim(outer_next, replica // 2, 1, 0)
    own_momentum = lax.dynamic_slice_in_dim(momentum_next, replica // 2, 1, 0)
    outer_other = permute(outer_next, core_swap)
    outer_pair = jnp.where(
        core == 0,
        jnp.stack([outer_next, outer_other], axis=1),
        jnp.stack([outer_other, outer_next], axis=1),
    )
    mix_alpha = (mix_step[0].astype(jnp.float32) + 1.0) / (MIXSTEPS + 1.0)
    new_inner = mix_alpha * outer_pair + (1.0 - mix_alpha) * inner_row.astype(jnp.float32)
    new_inner = new_inner.astype(jnp.bfloat16).reshape(1, -1)

    w_other = permute(w_half, core_swap)
    out = jax.ShapeDtypeStruct((tokens.shape[0], hd), jnp.bfloat16)
    first = pl.pallas_call(
        keys_first, out_shape=jax.ShapeDtypeStruct(out.shape, jnp.float32)
    )(tokens, w_half)
    key_out = pl.pallas_call(keys_second, out_shape=out)(tokens, w_other, inv, first)

    factor = jnp.sum(mine.astype(jnp.float32), axis=0).T
    weight_grad = norm_gain.astype(jnp.float32)[:, None] * factor
    gain_grad = jnp.sum(key_weight.astype(jnp.float32) * factor, axis=1)
    return (key_out, weight_grad[None], gain_grad[None], own_outer, own_momentum, new_inner[None])


def solution(mesh):
    in_specs = (
        P(("replica", "fsdp"), None),
        P("fsdp"),
        P("fsdp", None),
        P(("replica", "fsdp"), None),
        P(None, "fsdp", None),
        P(None, "fsdp", None),
        P("replica", None, "fsdp", None),
        P(),
        P("replica"),
    )
    out_specs = (
        P(("replica", "fsdp"), None),
        P("replica", "fsdp", None),
        P("replica", "fsdp"),
        P("fsdp", "replica"),
        P("fsdp", "replica"),
        P("replica", "fsdp", None),
    )
    return jax.shard_map(step, mesh=mesh, in_specs=in_specs, out_specs=out_specs, check_vma=False)
```

```python
import jax
import jax.numpy as jnp
from jax import lax
from jax.experimental import pallas as pl
from jax.experimental.pallas import tpu as pltpu
from jax.sharding import PartitionSpec as P


MIXSTEPS = 8
ALL = ("replica", "fsdp")
VMEM = pl.BlockSpec(memory_space=pltpu.VMEM)

norm_eps = 1e-05


def on_chip(*values):
    return [pltpu.with_memory_space_constraint(v, pltpu.VMEM) for v in values]


def route(move):
    pairs = []
    for r in range(64):
        for f in range(16):
            z, y, c, x = r // 8, (r // 2) % 4 + 4 * (f % 2), r % 2, f // 2
            z, y, c, x = move(z, y, c, x)
            pairs.append((r * 16 + f, (z * 8 + y % 4 * 2 + c) * 16 + x * 2 + y // 4))
    return pairs


def permute(value, move):
    return lax.ppermute(value, ALL, route(move))


def other_pair(i, n):
    return (i + 1) % n if i % 2 else (i - 1) % n


def x_near(z, y, c, x):
    return z, y, c, x ^ 1


def x_near_other(z, y, c, x):
    return z, y, c, other_pair(x, 8)


def y_one(z, y, c, x):
    return z, y ^ 1, c, x


def y_two(z, y, c, x):
    return z, y ^ 2, c, x


def z_one(z, y, c, x):
    return z ^ 1, y, c, x


def z_two(z, y, c, x):
    return z ^ 2, y, c, x


def z_four(z, y, c, x):
    return z ^ 4, y, c, x


def core_swap(z, y, c, x):
    return z, y, 1 - c, x


def factor_kernel(tok_ref, cot_ref, inv_ref, keep_ref, send_a, send_b):
    tokens, width = tok_ref.shape
    chunk = keep_ref.shape[2]

    def squares(i, acc):
        for k in range(chunk // 128):
            t = tok_ref[:, pl.ds(pl.multiple_of(i * chunk + k * 128, 128), 128)].astype(jnp.float32)
            acc = acc + t * t
        return acc

    acc = lax.fori_loop(0, width // chunk, squares, jnp.zeros((tokens, 128), jnp.float32))
    inv = lax.rsqrt(jnp.sum(acc, axis=1, keepdims=True) / width + norm_eps)
    inv_ref[...] = jnp.broadcast_to(inv, inv_ref.shape)
    scaled = (cot_ref[...].astype(jnp.float32) * inv).T.astype(jnp.bfloat16)
    parity = (lax.axis_index("fsdp") // 2) % 2

    def product(slot, x0):
        source = ((slot // 2) * 2 + x0) * 2 + slot % 2
        columns = tok_ref[:, pl.ds(pl.multiple_of(source * chunk, chunk), chunk)]
        return jnp.dot(scaled, columns, preferred_element_type=jnp.float32).astype(jnp.bfloat16)

    for slot in range(8):
        (send_a, send_b)[slot // 4][slot % 4] = product(slot, 1 - parity)
        keep_ref[slot] = product(slot, parity)


def factor_parts(tokens, cot, chunk):
    hd = cot.shape[1]
    half = jax.ShapeDtypeStruct((4, hd, chunk), jnp.bfloat16)
    return pl.pallas_call(
        factor_kernel,
        out_shape=(
            jax.ShapeDtypeStruct((tokens.shape[0], 128), jnp.float32),
            jax.ShapeDtypeStruct((8, hd, chunk), jnp.bfloat16),
            half,
            half,
        ),
        in_specs=[VMEM] * 2,
        out_specs=(VMEM,) * 4,
    )(tokens, cot)


def add_kernel(keep_ref, a_ref, b_ref, out_ref):
    for slot in range(8):
        other = (a_ref, b_ref)[slot // 4][slot % 4]
        out_ref[slot] = (keep_ref[slot].astype(jnp.float32) + other.astype(jnp.float32)).astype(
            out_ref.dtype
        )


def add_parts(keep, a, b):
    return pl.pallas_call(
        add_kernel,
        out_shape=jax.ShapeDtypeStruct(keep.shape, keep.dtype),
        in_specs=[VMEM] * 3,
        out_specs=VMEM,
    )(*on_chip(keep, a, b))


def keys_product(tok_ref, w_refs, flip):
    groups, shards, piece, hd = w_refs[0].shape
    rows = groups * piece
    replica = lax.axis_index("replica")
    half = (replica + flip) % 2
    acc = jnp.zeros((tok_ref.shape[0], hd), jnp.float32)
    for f in range(shards):
        for other, w_ref in enumerate(w_refs):
            quarter = (replica // 8 + other) % 2
            start = pl.multiple_of(((f * 2 + half) * 2 + quarter) * rows, rows)
            acc = acc + jnp.dot(
                tok_ref[:, pl.ds(start, rows)],
                w_ref[:, f].reshape(rows, hd),
                preferred_element_type=jnp.float32,
            )
    return acc


def keys_first(tok_ref, near_ref, far_ref, out_ref):
    out_ref[...] = keys_product(tok_ref, (near_ref, far_ref), 0)


def keys_second(tok_ref, near_ref, far_ref, inv_ref, first_ref, out_ref):
    acc = first_ref[...] + keys_product(tok_ref, (near_ref, far_ref), 1)
    out_ref[...] = (acc * inv_ref[...]).astype(out_ref.dtype)


def step(
    tokens,
    norm_gain,
    key_weight,
    key_cotangent,
    outer_params,
    outer_momentum,
    inner_params,
    fragment,
    mix_step,
):
    rows, hd = key_weight.shape
    replica = lax.axis_index("replica")
    replicas = lax.axis_size("replica")
    core = replica % 2

    inv, keep, send_a, send_b = factor_parts(tokens, key_cotangent, rows)
    recv_a = permute(send_a, x_near)
    recv_b = permute(send_b, x_near_other)

    plane = replica // 8
    piece = rows // 16
    z_bits = (plane // 4, plane // 2 % 2, plane % 2)
    order = core * 8 + z_bits[2] * 4 + z_bits[1] * 2 + z_bits[0]
    gain_piece = lax.dynamic_slice_in_dim(norm_gain, order * piece, piece, 0).astype(jnp.float32)
    weight_piece = lax.dynamic_slice_in_dim(key_weight, order * piece, piece, 0).astype(jnp.float32)
    scaled_piece = (gain_piece[:, None] * weight_piece).astype(jnp.bfloat16)
    shards = lax.axis_size("fsdp")
    w_pieces = lax.all_to_all(
        jnp.broadcast_to(scaled_piece[None], (shards, piece, hd)), "fsdp", 0, 0
    )[None]

    def doubled(values, move, bit):
        other = permute(values, move)
        return jnp.concatenate(
            [jnp.where(bit == 0, values, other), jnp.where(bit == 0, other, values)]
        )

    w_pieces = doubled(w_pieces, z_four, z_bits[0])
    w_near = doubled(w_pieces, z_two, z_bits[1])
    w_far = permute(w_near, z_one)
    w_near_other = permute(w_near, core_swap)
    w_far_other = permute(w_far, core_swap)
    part = add_parts(keep, recv_a, recv_b)
    x_groups = [[4 * k + 2 * p + y for k in range(4) for y in range(2)] for p in range(2)]
    mine = lax.all_to_all(part, "fsdp", 0, 0, axis_index_groups=x_groups)

    blocks = (replicas // 2, 2, outer_params.shape[2] // replicas)

    def row_of(values):
        return lax.dynamic_index_in_dim(values, fragment, 0, keepdims=False).reshape(blocks)

    def half_of(values):
        return lax.dynamic_index_in_dim(values, core, 1, keepdims=False)

    inner_row = row_of(inner_params[0])
    other_core = permute(
        lax.dynamic_index_in_dim(inner_row, 1 - core, 1, keepdims=False), core_swap
    )
    total = half_of(inner_row).astype(jnp.float32) + other_core.astype(jnp.float32)
    for move in (y_one, y_two, z_one, z_two, z_four):
        total = total + permute(total, move)
    outer_now = half_of(row_of(outer_params))
    momentum_now = half_of(row_of(outer_momentum))
    pseudo_grad = outer_now - total / replicas
    momentum_next = 0.9 * momentum_now + pseudo_grad
    outer_next = outer_now - 0.7 * (pseudo_grad + 0.9 * momentum_next)
    own_outer = lax.dynamic_slice_in_dim(outer_next, replica // 2, 1, 0)
    own_momentum = lax.dynamic_slice_in_dim(momentum_next, replica // 2, 1, 0)
    outer_other = permute(outer_next, core_swap)
    outer_pair = jnp.where(
        core == 0,
        jnp.stack([outer_next, outer_other], axis=1),
        jnp.stack([outer_other, outer_next], axis=1),
    )
    mix_alpha = (mix_step[0].astype(jnp.float32) + 1.0) / (MIXSTEPS + 1.0)
    new_inner = mix_alpha * outer_pair + (1.0 - mix_alpha) * inner_row.astype(jnp.float32)
    new_inner = new_inner.astype(jnp.bfloat16).reshape(1, -1)

    out = jax.ShapeDtypeStruct((tokens.shape[0], hd), jnp.bfloat16)
    first = pl.pallas_call(
        keys_first,
        out_shape=jax.ShapeDtypeStruct(out.shape, jnp.float32),
        in_specs=[VMEM] * 3,
        out_specs=VMEM,
    )(tokens, *on_chip(w_near, w_far))
    key_out = pl.pallas_call(
        keys_second, out_shape=out, in_specs=[VMEM] * 5, out_specs=VMEM
    )(tokens, *on_chip(w_near_other, w_far_other, inv, first))

    factor = jnp.sum(mine.astype(jnp.float32), axis=0).T
    weight_grad = norm_gain.astype(jnp.float32)[:, None] * factor
    gain_grad = jnp.sum(key_weight.astype(jnp.float32) * factor, axis=1)
    return (key_out, weight_grad[None], gain_grad[None], own_outer, own_momentum, new_inner[None])


def solution(mesh):
    in_specs = (
        P(("replica", "fsdp"), None),
        P("fsdp"),
        P("fsdp", None),
        P(("replica", "fsdp"), None),
        P(None, "fsdp", None),
        P(None, "fsdp", None),
        P("replica", None, "fsdp", None),
        P(),
        P("replica"),
    )
    out_specs = (
        P(("replica", "fsdp"), None),
        P("replica", "fsdp", None),
        P("replica", "fsdp"),
        P("fsdp", "replica"),
        P("fsdp", "replica"),
        P("replica", "fsdp", None),
    )
    return jax.shard_map(step, mesh=mesh, in_specs=in_specs, out_specs=out_specs, check_vma=False)
```

```python
import jax
import jax.numpy as jnp
from jax import lax
from jax.experimental import pallas as pl
from jax.experimental.pallas import tpu as pltpu
from jax.sharding import PartitionSpec as P


MIXSTEPS = 8
ALL = ("replica", "fsdp")
VMEM = pl.BlockSpec(memory_space=pltpu.VMEM)

norm_eps = 1e-05


def on_chip(*values):
    return [pltpu.with_memory_space_constraint(v, pltpu.VMEM) for v in values]


def route(move):
    pairs = []
    for r in range(64):
        for f in range(16):
            z, y, c, x = r // 8, (r // 2) % 4 + 4 * (f % 2), r % 2, f // 2
            z, y, c, x = move(z, y, c, x)
            pairs.append((r * 16 + f, (z * 8 + y % 4 * 2 + c) * 16 + x * 2 + y // 4))
    return pairs


def permute(value, move):
    return lax.ppermute(value, ALL, route(move))


def other_pair(i, n):
    return (i + 1) % n if i % 2 else (i - 1) % n


def x_near(z, y, c, x):
    return z, y, c, x ^ 1


def x_near_other(z, y, c, x):
    return z, y, c, other_pair(x, 8)


def z_one(z, y, c, x):
    return z ^ 1, y, c, x


def z_two(z, y, c, x):
    return z ^ 2, y, c, x


def z_four(z, y, c, x):
    return z ^ 4, y, c, x


def core_swap(z, y, c, x):
    return z, y, 1 - c, x


def factor_kernel(tok_ref, cot_ref, inv_ref, keep_ref, send_a, send_b):
    tokens, width = tok_ref.shape
    chunk = keep_ref.shape[2]

    def squares(i, acc):
        for k in range(chunk // 128):
            t = tok_ref[:, pl.ds(pl.multiple_of(i * chunk + k * 128, 128), 128)].astype(jnp.float32)
            acc = acc + t * t
        return acc

    acc = lax.fori_loop(0, width // chunk, squares, jnp.zeros((tokens, 128), jnp.float32))
    inv = lax.rsqrt(jnp.sum(acc, axis=1, keepdims=True) / width + norm_eps)
    inv_ref[...] = jnp.broadcast_to(inv, inv_ref.shape)
    scaled = (cot_ref[...].astype(jnp.float32) * inv).T.astype(jnp.bfloat16)
    parity = (lax.axis_index("fsdp") // 2) % 2

    def product(slot, x0):
        source = ((slot // 2) * 2 + x0) * 2 + slot % 2
        columns = tok_ref[:, pl.ds(pl.multiple_of(source * chunk, chunk), chunk)]
        return jnp.dot(scaled, columns, preferred_element_type=jnp.float32).astype(jnp.bfloat16)

    for slot in range(8):
        (send_a, send_b)[slot // 4][slot % 4] = product(slot, 1 - parity)
        keep_ref[slot] = product(slot, parity)


def factor_parts(tokens, cot, chunk):
    hd = cot.shape[1]
    half = pltpu.VMEM((4, hd, chunk), jnp.bfloat16)
    return pl.pallas_call(
        factor_kernel,
        out_shape=(
            pltpu.VMEM((tokens.shape[0], 128), jnp.float32),
            pltpu.VMEM((8, hd, chunk), jnp.bfloat16),
            half,
            half,
        ),
        in_specs=[VMEM] * 2,
        out_specs=(VMEM,) * 4,
    )(tokens, cot)


def add_kernel(keep_ref, a_ref, b_ref, out_ref):
    for slot in range(8):
        other = (a_ref, b_ref)[slot // 4][slot % 4]
        out_ref[slot] = (keep_ref[slot].astype(jnp.float32) + other.astype(jnp.float32)).astype(
            out_ref.dtype
        )


def add_parts(keep, a, b):
    return pl.pallas_call(
        add_kernel,
        out_shape=jax.ShapeDtypeStruct(keep.shape, keep.dtype),
        in_specs=[VMEM] * 3,
        out_specs=VMEM,
    )(*on_chip(keep, a, b))


def keys_product(tok_ref, w_refs, flip):
    groups, shards, piece, hd = w_refs[0].shape
    rows = groups * piece
    replica = lax.axis_index("replica")
    half = (replica + flip) % 2
    acc = jnp.zeros((tok_ref.shape[0], hd), jnp.float32)
    for f in range(shards):
        for other, w_ref in enumerate(w_refs):
            quarter = (replica // 8 + other) % 2
            start = pl.multiple_of(((f * 2 + half) * 2 + quarter) * rows, rows)
            acc = acc + jnp.dot(
                tok_ref[:, pl.ds(start, rows)],
                w_ref[:, f].reshape(rows, hd),
                preferred_element_type=jnp.float32,
            )
    return acc


def keys_first(tok_ref, near_ref, far_ref, out_ref):
    out_ref[...] = keys_product(tok_ref, (near_ref, far_ref), 0)


def keys_second(tok_ref, near_ref, far_ref, inv_ref, first_ref, out_ref):
    acc = first_ref[...] + keys_product(tok_ref, (near_ref, far_ref), 1)
    out_ref[...] = (acc * inv_ref[...]).astype(out_ref.dtype)


def step(
    tokens,
    norm_gain,
    key_weight,
    key_cotangent,
    outer_params,
    outer_momentum,
    inner_params,
    fragment,
    mix_step,
):
    rows, hd = key_weight.shape
    replica = lax.axis_index("replica")
    replicas = lax.axis_size("replica")
    core = replica % 2

    inv, keep, send_a, send_b = factor_parts(tokens, key_cotangent, rows)
    recv_a = permute(send_a, x_near)
    recv_b = permute(send_b, x_near_other)

    plane = replica // 8
    piece = rows // 16
    z_bits = (plane // 4, plane // 2 % 2, plane % 2)
    order = core * 8 + z_bits[2] * 4 + z_bits[1] * 2 + z_bits[0]
    gain_piece = lax.dynamic_slice_in_dim(norm_gain, order * piece, piece, 0).astype(jnp.float32)
    weight_piece = lax.dynamic_slice_in_dim(key_weight, order * piece, piece, 0).astype(jnp.float32)
    scaled_piece = (gain_piece[:, None] * weight_piece).astype(jnp.bfloat16)
    shards = lax.axis_size("fsdp")
    w_pieces = lax.all_to_all(
        jnp.broadcast_to(scaled_piece[None], (shards, piece, hd)), "fsdp", 0, 0
    )[None]

    def doubled(values, move, bit):
        other = permute(values, move)
        return jnp.concatenate(
            [jnp.where(bit == 0, values, other), jnp.where(bit == 0, other, values)]
        )

    w_pieces = doubled(w_pieces, z_four, z_bits[0])
    w_near = doubled(w_pieces, z_two, z_bits[1])
    w_far = permute(w_near, z_one)
    w_near_other = permute(w_near, core_swap)
    w_far_other = permute(w_far, core_swap)
    part = add_parts(keep, recv_a, recv_b)
    x_groups = [[4 * k + 2 * p + y for k in range(4) for y in range(2)] for p in range(2)]
    mine = lax.all_to_all(part, "fsdp", 0, 0, axis_index_groups=x_groups)

    blocks = (replicas // 2, 2, outer_params.shape[2] // replicas)

    def row_of(values):
        return lax.dynamic_index_in_dim(values, fragment, 0, keepdims=False).reshape(blocks)

    def half_of(values):
        return lax.dynamic_index_in_dim(values, core, 1, keepdims=False)

    inner_row = row_of(inner_params[0])
    halves = jnp.broadcast_to(
        inner_row.transpose(1, 0, 2)[None], (replicas // 2, 2, blocks[0], blocks[2])
    ).reshape(replicas, blocks[0], blocks[2])
    inner_all = lax.all_to_all(halves, "replica", 0, 0)
    total = jnp.sum(inner_all.astype(jnp.float32), axis=0)
    outer_now = half_of(row_of(outer_params))
    momentum_now = half_of(row_of(outer_momentum))
    pseudo_grad = outer_now - total / replicas
    momentum_next = 0.9 * momentum_now + pseudo_grad
    outer_next = outer_now - 0.7 * (pseudo_grad + 0.9 * momentum_next)
    own_outer = lax.dynamic_slice_in_dim(outer_next, replica // 2, 1, 0)
    own_momentum = lax.dynamic_slice_in_dim(momentum_next, replica // 2, 1, 0)
    outer_other = permute(outer_next, core_swap)
    outer_pair = jnp.where(
        core == 0,
        jnp.stack([outer_next, outer_other], axis=1),
        jnp.stack([outer_other, outer_next], axis=1),
    )
    mix_alpha = (mix_step[0].astype(jnp.float32) + 1.0) / (MIXSTEPS + 1.0)
    new_inner = mix_alpha * outer_pair + (1.0 - mix_alpha) * inner_row.astype(jnp.float32)
    new_inner = new_inner.astype(jnp.bfloat16).reshape(1, -1)

    out = jax.ShapeDtypeStruct((tokens.shape[0], hd), jnp.bfloat16)
    first = pl.pallas_call(
        keys_first,
        out_shape=pltpu.VMEM(out.shape, jnp.float32),
        in_specs=[VMEM] * 3,
        out_specs=VMEM,
    )(tokens, *on_chip(w_near, w_far))
    key_out = pl.pallas_call(
        keys_second, out_shape=out, in_specs=[VMEM] * 5, out_specs=VMEM
    )(tokens, *on_chip(w_near_other, w_far_other, inv, first))

    factor = jnp.sum(mine.astype(jnp.float32), axis=0).T
    weight_grad = norm_gain.astype(jnp.float32)[:, None] * factor
    gain_grad = jnp.sum(key_weight.astype(jnp.float32) * factor, axis=1)
    return (key_out, weight_grad[None], gain_grad[None], own_outer, own_momentum, new_inner[None])


def solution(mesh):
    in_specs = (
        P(("replica", "fsdp"), None),
        P("fsdp"),
        P("fsdp", None),
        P(("replica", "fsdp"), None),
        P(None, "fsdp", None),
        P(None, "fsdp", None),
        P("replica", None, "fsdp", None),
        P(),
        P("replica"),
    )
    out_specs = (
        P(("replica", "fsdp"), None),
        P("replica", "fsdp", None),
        P("replica", "fsdp"),
        P("fsdp", "replica"),
        P("fsdp", "replica"),
        P("replica", "fsdp", None),
    )
    return jax.shard_map(step, mesh=mesh, in_specs=in_specs, out_specs=out_specs, check_vma=False)
```

```python
import jax
import jax.numpy as jnp
from jax import lax
from jax.experimental import pallas as pl
from jax.experimental.pallas import tpu as pltpu
from jax.sharding import PartitionSpec as P


MIXSTEPS = 8
ALL = ("replica", "fsdp")
VMEM = pl.BlockSpec(memory_space=pltpu.VMEM)

norm_eps = 1e-05


def on_chip(*values):
    return [pltpu.with_memory_space_constraint(v, pltpu.VMEM) for v in values]


def route(move):
    pairs = []
    for r in range(64):
        for f in range(16):
            z, y, c, x = r // 8, (r // 2) % 4 + 4 * (f % 2), r % 2, f // 2
            z, y, c, x = move(z, y, c, x)
            pairs.append((r * 16 + f, (z * 8 + y % 4 * 2 + c) * 16 + x * 2 + y // 4))
    return pairs


def permute(value, move):
    return lax.ppermute(value, ALL, route(move))


def x_near(z, y, c, x):
    return z, y, c, (x + (1 if (x + c) % 2 == 0 else -1)) % 8


def z_one(z, y, c, x):
    return z ^ 1, y, c, x


def z_two(z, y, c, x):
    return z ^ 2, y, c, x


def z_four(z, y, c, x):
    return z ^ 4, y, c, x


def core_swap(z, y, c, x):
    return z, y, 1 - c, x


def factor_kernel(tok_ref, cot_ref, inv_ref, keep_ref, send_ref):
    tokens, width = tok_ref.shape
    chunk = keep_ref.shape[2]

    def squares(i, acc):
        for k in range(chunk // 128):
            t = tok_ref[:, pl.ds(pl.multiple_of(i * chunk + k * 128, 128), 128)].astype(jnp.float32)
            acc = acc + t * t
        return acc

    acc = lax.fori_loop(0, width // chunk, squares, jnp.zeros((tokens, 128), jnp.float32))
    inv = lax.rsqrt(jnp.sum(acc, axis=1, keepdims=True) / width + norm_eps)
    inv_ref[...] = jnp.broadcast_to(inv, inv_ref.shape)
    scaled = (cot_ref[...].astype(jnp.float32) * inv).T.astype(jnp.bfloat16)
    parity = (lax.axis_index("fsdp") // 2) % 2

    def product(slot, x0):
        source = ((slot // 2) * 2 + x0) * 2 + slot % 2
        columns = tok_ref[:, pl.ds(pl.multiple_of(source * chunk, chunk), chunk)]
        return jnp.dot(scaled, columns, preferred_element_type=jnp.float32).astype(jnp.bfloat16)

    for slot in range(8):
        send_ref[slot] = product(slot, 1 - parity)
        keep_ref[slot] = product(slot, parity)


def factor_parts(tokens, cot, chunk):
    hd = cot.shape[1]
    return pl.pallas_call(
        factor_kernel,
        out_shape=(
            pltpu.VMEM((tokens.shape[0], 128), jnp.float32),
            pltpu.VMEM((8, hd, chunk), jnp.bfloat16),
            pltpu.VMEM((8, hd, chunk), jnp.bfloat16),
        ),
        in_specs=[VMEM] * 2,
        out_specs=(VMEM,) * 3,
    )(tokens, cot)


def add_kernel(keep_ref, other_ref, out_ref):
    for slot in range(8):
        total = keep_ref[slot].astype(jnp.float32) + other_ref[slot].astype(jnp.float32)
        out_ref[slot] = total.astype(out_ref.dtype)


def add_parts(keep, other):
    return pl.pallas_call(
        add_kernel,
        out_shape=jax.ShapeDtypeStruct(keep.shape, keep.dtype),
        in_specs=[VMEM] * 2,
        out_specs=VMEM,
    )(*on_chip(keep, other))


def keys_product(tok_ref, w_refs, flip):
    groups, shards, piece, hd = w_refs[0].shape
    rows = groups * piece
    replica = lax.axis_index("replica")
    half = (replica + flip) % 2
    acc = jnp.zeros((tok_ref.shape[0], hd), jnp.float32)
    for f in range(shards):
        for other, w_ref in enumerate(w_refs):
            quarter = (replica // 8 + other) % 2
            start = pl.multiple_of(((f * 2 + half) * 2 + quarter) * rows, rows)
            acc = acc + jnp.dot(
                tok_ref[:, pl.ds(start, rows)],
                w_ref[:, f].reshape(rows, hd),
                preferred_element_type=jnp.float32,
            )
    return acc


def keys_first(tok_ref, near_ref, far_ref, out_ref):
    out_ref[...] = keys_product(tok_ref, (near_ref, far_ref), 0)


def keys_second(tok_ref, near_ref, far_ref, inv_ref, first_ref, out_ref):
    acc = first_ref[...] + keys_product(tok_ref, (near_ref, far_ref), 1)
    out_ref[...] = (acc * inv_ref[...]).astype(out_ref.dtype)


def step(
    tokens,
    norm_gain,
    key_weight,
    key_cotangent,
    outer_params,
    outer_momentum,
    inner_params,
    fragment,
    mix_step,
):
    rows, hd = key_weight.shape
    replica = lax.axis_index("replica")
    replicas = lax.axis_size("replica")
    core = replica % 2

    inv, keep, send = factor_parts(tokens, key_cotangent, rows)
    recv = permute(send, x_near)

    plane = replica // 8
    piece = rows // 16
    z_bits = (plane // 4, plane // 2 % 2, plane % 2)
    order = core * 8 + z_bits[2] * 4 + z_bits[1] * 2 + z_bits[0]
    gain_piece = lax.dynamic_slice_in_dim(norm_gain, order * piece, piece, 0).astype(jnp.float32)
    weight_piece = lax.dynamic_slice_in_dim(key_weight, order * piece, piece, 0).astype(jnp.float32)
    scaled_piece = (gain_piece[:, None] * weight_piece).astype(jnp.bfloat16)
    shards = lax.axis_size("fsdp")
    w_pieces = lax.all_to_all(
        jnp.broadcast_to(scaled_piece[None], (shards, piece, hd)), "fsdp", 0, 0
    )[None]

    def doubled(values, move, bit):
        other = permute(values, move)
        return jnp.concatenate(
            [jnp.where(bit == 0, values, other), jnp.where(bit == 0, other, values)]
        )

    w_pieces = doubled(w_pieces, z_four, z_bits[0])
    w_near = doubled(w_pieces, z_two, z_bits[1])
    w_far = permute(w_near, z_one)
    w_near_other = permute(w_near, core_swap)
    w_far_other = permute(w_far, core_swap)
    part = add_parts(keep, recv)
    x_groups = [[4 * k + 2 * p + y for k in range(4) for y in range(2)] for p in range(2)]
    mine = lax.all_to_all(part, "fsdp", 0, 0, axis_index_groups=x_groups)

    blocks = (replicas // 2, 2, outer_params.shape[2] // replicas)

    def row_of(values):
        return lax.dynamic_index_in_dim(values, fragment, 0, keepdims=False).reshape(blocks)

    def half_of(values):
        return lax.dynamic_index_in_dim(values, core, 1, keepdims=False)

    inner_row = row_of(inner_params[0])
    halves = jnp.broadcast_to(
        inner_row.transpose(1, 0, 2)[None], (replicas // 2, 2, blocks[0], blocks[2])
    ).reshape(replicas, blocks[0], blocks[2])
    inner_all = lax.all_to_all(halves, "replica", 0, 0)
    total = jnp.sum(inner_all.astype(jnp.float32), axis=0)
    outer_now = half_of(row_of(outer_params))
    momentum_now = half_of(row_of(outer_momentum))
    pseudo_grad = outer_now - total / replicas
    momentum_next = 0.9 * momentum_now + pseudo_grad
    outer_next = outer_now - 0.7 * (pseudo_grad + 0.9 * momentum_next)
    own_outer = lax.dynamic_slice_in_dim(outer_next, replica // 2, 1, 0)
    own_momentum = lax.dynamic_slice_in_dim(momentum_next, replica // 2, 1, 0)
    outer_other = permute(outer_next, core_swap)
    outer_pair = jnp.where(
        core == 0,
        jnp.stack([outer_next, outer_other], axis=1),
        jnp.stack([outer_other, outer_next], axis=1),
    )
    mix_alpha = (mix_step[0].astype(jnp.float32) + 1.0) / (MIXSTEPS + 1.0)
    new_inner = mix_alpha * outer_pair + (1.0 - mix_alpha) * inner_row.astype(jnp.float32)
    new_inner = new_inner.astype(jnp.bfloat16).reshape(1, -1)

    out = jax.ShapeDtypeStruct((tokens.shape[0], hd), jnp.bfloat16)
    first = pl.pallas_call(
        keys_first,
        out_shape=pltpu.VMEM(out.shape, jnp.float32),
        in_specs=[VMEM] * 3,
        out_specs=VMEM,
    )(tokens, *on_chip(w_near, w_far))
    key_out = pl.pallas_call(
        keys_second, out_shape=out, in_specs=[VMEM] * 5, out_specs=VMEM
    )(tokens, *on_chip(w_near_other, w_far_other, inv, first))

    factor = jnp.sum(mine.astype(jnp.float32), axis=0).T
    weight_grad = norm_gain.astype(jnp.float32)[:, None] * factor
    gain_grad = jnp.sum(key_weight.astype(jnp.float32) * factor, axis=1)
    return (key_out, weight_grad[None], gain_grad[None], own_outer, own_momentum, new_inner[None])


def solution(mesh):
    in_specs = (
        P(("replica", "fsdp"), None),
        P("fsdp"),
        P("fsdp", None),
        P(("replica", "fsdp"), None),
        P(None, "fsdp", None),
        P(None, "fsdp", None),
        P("replica", None, "fsdp", None),
        P(),
        P("replica"),
    )
    out_specs = (
        P(("replica", "fsdp"), None),
        P("replica", "fsdp", None),
        P("replica", "fsdp"),
        P("fsdp", "replica"),
        P("fsdp", "replica"),
        P("replica", "fsdp", None),
    )
    return jax.shard_map(step, mesh=mesh, in_specs=in_specs, out_specs=out_specs, check_vma=False)
```

```python
import jax
import jax.numpy as jnp
from jax import lax
from jax.experimental import pallas as pl
from jax.experimental.pallas import tpu as pltpu
from jax.sharding import PartitionSpec as P


MIXSTEPS = 8
ALL = ("replica", "fsdp")
VMEM = pl.BlockSpec(memory_space=pltpu.VMEM)

norm_eps = 1e-05


def on_chip(*values):
    return [pltpu.with_memory_space_constraint(v, pltpu.VMEM) for v in values]


def route(move):
    pairs = []
    for r in range(64):
        for f in range(16):
            z, y, c, x = r // 8, (r // 2) % 4 + 4 * (f % 2), r % 2, f // 2
            z, y, c, x = move(z, y, c, x)
            pairs.append((r * 16 + f, (z * 8 + y % 4 * 2 + c) * 16 + x * 2 + y // 4))
    return pairs


def permute(value, move):
    return lax.ppermute(value, ALL, route(move))


def x_near(z, y, c, x):
    return z, y, c, (x + (1 if (x + c) % 2 == 0 else -1)) % 8


def y_half(z, y, c, x):
    return z, (6, 7, 4, 5, 2, 3, 0, 1)[y], c, x


def z_one(z, y, c, x):
    return z ^ 1, y, c, x


def z_two(z, y, c, x):
    return z ^ 2, y, c, x


def z_four(z, y, c, x):
    return z ^ 4, y, c, x


def core_swap(z, y, c, x):
    return z, y, 1 - c, x


def factor_kernel(tok_ref, cot_ref, inv_ref, keep_ref, send_ref):
    tokens, width = tok_ref.shape
    chunk = keep_ref.shape[2]

    def squares(i, acc):
        for k in range(chunk // 128):
            t = tok_ref[:, pl.ds(pl.multiple_of(i * chunk + k * 128, 128), 128)].astype(jnp.float32)
            acc = acc + t * t
        return acc

    acc = lax.fori_loop(0, width // chunk, squares, jnp.zeros((tokens, 128), jnp.float32))
    inv = lax.rsqrt(jnp.sum(acc, axis=1, keepdims=True) / width + norm_eps)
    inv_ref[...] = jnp.broadcast_to(inv, inv_ref.shape)
    scaled = (cot_ref[...].astype(jnp.float32) * inv).T.astype(jnp.bfloat16)
    parity = (lax.axis_index("fsdp") // 2) % 2

    def product(slot, x0):
        source = ((slot // 2) * 2 + x0) * 2 + slot % 2
        columns = tok_ref[:, pl.ds(pl.multiple_of(source * chunk, chunk), chunk)]
        return jnp.dot(scaled, columns, preferred_element_type=jnp.float32).astype(jnp.bfloat16)

    for slot in range(8):
        send_ref[slot] = product(slot, 1 - parity)
        keep_ref[slot] = product(slot, parity)


def factor_parts(tokens, cot, chunk):
    hd = cot.shape[1]
    return pl.pallas_call(
        factor_kernel,
        out_shape=(
            pltpu.VMEM((tokens.shape[0], 128), jnp.float32),
            pltpu.VMEM((8, hd, chunk), jnp.bfloat16),
            pltpu.VMEM((8, hd, chunk), jnp.bfloat16),
        ),
        in_specs=[VMEM] * 2,
        out_specs=(VMEM,) * 3,
    )(tokens, cot)


def add_kernel(keep_ref, other_ref, out_ref):
    for slot in range(8):
        total = keep_ref[slot].astype(jnp.float32) + other_ref[slot].astype(jnp.float32)
        out_ref[slot] = total.astype(out_ref.dtype)


def add_parts(keep, other):
    return pl.pallas_call(
        add_kernel,
        out_shape=jax.ShapeDtypeStruct(keep.shape, keep.dtype),
        in_specs=[VMEM] * 2,
        out_specs=VMEM,
    )(*on_chip(keep, other))


def keys_product(tok_ref, w_refs, flip):
    groups, shards, piece, hd = w_refs[0].shape
    rows = groups * piece
    replica = lax.axis_index("replica")
    half = (replica + flip) % 2
    y_half_index = lax.axis_index("fsdp") % 2
    acc = jnp.zeros((tok_ref.shape[0], hd), jnp.float32)
    for f in range(shards):
        shard = (f % 8) * 2 + (y_half_index + f // 8) % 2
        for other, w_ref in enumerate(w_refs):
            quarter = (replica // 8 + other) % 2
            start = pl.multiple_of(((shard * 2 + half) * 2 + quarter) * rows, rows)
            acc = acc + jnp.dot(
                tok_ref[:, pl.ds(start, rows)],
                w_ref[:, f].reshape(rows, hd),
                preferred_element_type=jnp.float32,
            )
    return acc


def keys_first(tok_ref, near_ref, far_ref, out_ref):
    out_ref[...] = keys_product(tok_ref, (near_ref, far_ref), 0)


def keys_second(tok_ref, near_ref, far_ref, inv_ref, first_ref, out_ref):
    acc = first_ref[...] + keys_product(tok_ref, (near_ref, far_ref), 1)
    out_ref[...] = (acc * inv_ref[...]).astype(out_ref.dtype)


def step(
    tokens,
    norm_gain,
    key_weight,
    key_cotangent,
    outer_params,
    outer_momentum,
    inner_params,
    fragment,
    mix_step,
):
    rows, hd = key_weight.shape
    replica = lax.axis_index("replica")
    replicas = lax.axis_size("replica")
    core = replica % 2

    inv, keep, send = factor_parts(tokens, key_cotangent, rows)
    recv = permute(send, x_near)

    plane = replica // 8
    piece = rows // 16
    z_bits = (plane // 4, plane // 2 % 2, plane % 2)
    order = core * 8 + z_bits[2] * 4 + z_bits[1] * 2 + z_bits[0]
    gain_piece = lax.dynamic_slice_in_dim(norm_gain, order * piece, piece, 0).astype(jnp.float32)
    weight_piece = lax.dynamic_slice_in_dim(key_weight, order * piece, piece, 0).astype(jnp.float32)
    scaled_piece = (gain_piece[:, None] * weight_piece).astype(jnp.bfloat16)
    y_groups = [[2 * x + y for x in range(8)] for y in range(2)]
    w_row = lax.all_to_all(
        jnp.broadcast_to(scaled_piece[None], (8, piece, hd)),
        "fsdp",
        0,
        0,
        axis_index_groups=y_groups,
    )
    w_pieces = jnp.concatenate([w_row, permute(w_row, y_half)])[None]

    def doubled(values, move, bit):
        other = permute(values, move)
        return jnp.concatenate(
            [jnp.where(bit == 0, values, other), jnp.where(bit == 0, other, values)]
        )

    w_pieces = doubled(w_pieces, z_four, z_bits[0])
    w_near = doubled(w_pieces, z_two, z_bits[1])
    w_far = permute(w_near, z_one)
    w_near_other = permute(w_near, core_swap)
    w_far_other = permute(w_far, core_swap)
    part = add_parts(keep, recv)
    x_groups = [[4 * k + 2 * p + y for k in range(4) for y in range(2)] for p in range(2)]
    mine = lax.all_to_all(part, "fsdp", 0, 0, axis_index_groups=x_groups)

    blocks = (replicas // 2, 2, outer_params.shape[2] // replicas)

    def row_of(values):
        return lax.dynamic_index_in_dim(values, fragment, 0, keepdims=False).reshape(blocks)

    def half_of(values):
        return lax.dynamic_index_in_dim(values, core, 1, keepdims=False)

    inner_row = row_of(inner_params[0])
    halves = jnp.broadcast_to(
        inner_row.transpose(1, 0, 2)[None], (replicas // 2, 2, blocks[0], blocks[2])
    ).reshape(replicas, blocks[0], blocks[2])
    inner_all = lax.all_to_all(halves, "replica", 0, 0)
    total = jnp.sum(inner_all.astype(jnp.float32), axis=0)
    outer_now = half_of(row_of(outer_params))
    momentum_now = half_of(row_of(outer_momentum))
    pseudo_grad = outer_now - total / replicas
    momentum_next = 0.9 * momentum_now + pseudo_grad
    outer_next = outer_now - 0.7 * (pseudo_grad + 0.9 * momentum_next)
    own_outer = lax.dynamic_slice_in_dim(outer_next, replica // 2, 1, 0)
    own_momentum = lax.dynamic_slice_in_dim(momentum_next, replica // 2, 1, 0)
    outer_other = permute(outer_next, core_swap)
    outer_pair = jnp.where(
        core == 0,
        jnp.stack([outer_next, outer_other], axis=1),
        jnp.stack([outer_other, outer_next], axis=1),
    )
    mix_alpha = (mix_step[0].astype(jnp.float32) + 1.0) / (MIXSTEPS + 1.0)
    new_inner = mix_alpha * outer_pair + (1.0 - mix_alpha) * inner_row.astype(jnp.float32)
    new_inner = new_inner.astype(jnp.bfloat16).reshape(1, -1)

    out = jax.ShapeDtypeStruct((tokens.shape[0], hd), jnp.bfloat16)
    first = pl.pallas_call(
        keys_first,
        out_shape=pltpu.VMEM(out.shape, jnp.float32),
        in_specs=[VMEM] * 3,
        out_specs=VMEM,
    )(tokens, *on_chip(w_near, w_far))
    key_out = pl.pallas_call(
        keys_second, out_shape=out, in_specs=[VMEM] * 5, out_specs=VMEM
    )(tokens, *on_chip(w_near_other, w_far_other, inv, first))

    factor = jnp.sum(mine.astype(jnp.float32), axis=0).T
    weight_grad = norm_gain.astype(jnp.float32)[:, None] * factor
    gain_grad = jnp.sum(key_weight.astype(jnp.float32) * factor, axis=1)
    return (key_out, weight_grad[None], gain_grad[None], own_outer, own_momentum, new_inner[None])


def solution(mesh):
    in_specs = (
        P(("replica", "fsdp"), None),
        P("fsdp"),
        P("fsdp", None),
        P(("replica", "fsdp"), None),
        P(None, "fsdp", None),
        P(None, "fsdp", None),
        P("replica", None, "fsdp", None),
        P(),
        P("replica"),
    )
    out_specs = (
        P(("replica", "fsdp"), None),
        P("replica", "fsdp", None),
        P("replica", "fsdp"),
        P("fsdp", "replica"),
        P("fsdp", "replica"),
        P("replica", "fsdp", None),
    )
    return jax.shard_map(step, mesh=mesh, in_specs=in_specs, out_specs=out_specs, check_vma=False)
```

```python
import jax
import jax.numpy as jnp
from jax import lax
from jax.experimental import pallas as pl
from jax.experimental.pallas import tpu as pltpu
from jax.sharding import PartitionSpec as P


MIXSTEPS = 8
ALL = ("replica", "fsdp")
VMEM = pl.BlockSpec(memory_space=pltpu.VMEM)

norm_eps = 1e-05


def on_chip(*values):
    return [pltpu.with_memory_space_constraint(v, pltpu.VMEM) for v in values]


def route(move):
    pairs = []
    for r in range(64):
        for f in range(16):
            z, y, c, x = r // 8, (r // 2) % 4 + 4 * (f % 2), r % 2, f // 2
            z, y, c, x = move(z, y, c, x)
            pairs.append((r * 16 + f, (z * 8 + y % 4 * 2 + c) * 16 + x * 2 + y // 4))
    return pairs


def permute(value, move):
    return lax.ppermute(value, ALL, route(move))


def x_near(z, y, c, x):
    return z, y, c, (x + (1 if (x + c) % 2 == 0 else -1)) % 8


def y_half(z, y, c, x):
    return z, (6, 7, 4, 5, 2, 3, 0, 1)[y], c, x


def z_one(z, y, c, x):
    return (z + (1 if (z + c) % 2 == 0 else -1)) % 8, y, c, x


def z_two(z, y, c, x):
    return z ^ (6 if c else 2), y, c, x


def z_four(z, y, c, x):
    return z ^ 4, y, c, x


def core_swap(z, y, c, x):
    return z, y, 1 - c, x


def factor_kernel(tok_ref, cot_ref, inv_ref, keep_ref, send_ref):
    tokens, width = tok_ref.shape
    chunk = keep_ref.shape[2]

    def squares(i, acc):
        for k in range(chunk // 128):
            t = tok_ref[:, pl.ds(pl.multiple_of(i * chunk + k * 128, 128), 128)].astype(jnp.float32)
            acc = acc + t * t
        return acc

    acc = lax.fori_loop(0, width // chunk, squares, jnp.zeros((tokens, 128), jnp.float32))
    inv = lax.rsqrt(jnp.sum(acc, axis=1, keepdims=True) / width + norm_eps)
    inv_ref[...] = jnp.broadcast_to(inv, inv_ref.shape)
    scaled = (cot_ref[...].astype(jnp.float32) * inv).T.astype(jnp.bfloat16)
    parity = (lax.axis_index("fsdp") // 2) % 2

    def product(slot, x0):
        source = ((slot // 2) * 2 + x0) * 2 + slot % 2
        columns = tok_ref[:, pl.ds(pl.multiple_of(source * chunk, chunk), chunk)]
        return jnp.dot(scaled, columns, preferred_element_type=jnp.float32).astype(jnp.bfloat16)

    for slot in range(8):
        send_ref[slot] = product(slot, 1 - parity)
        keep_ref[slot] = product(slot, parity)


def factor_parts(tokens, cot, chunk):
    hd = cot.shape[1]
    return pl.pallas_call(
        factor_kernel,
        out_shape=(
            pltpu.VMEM((tokens.shape[0], 128), jnp.float32),
            pltpu.VMEM((8, hd, chunk), jnp.bfloat16),
            pltpu.VMEM((8, hd, chunk), jnp.bfloat16),
        ),
        in_specs=[VMEM] * 2,
        out_specs=(VMEM,) * 3,
    )(tokens, cot)


def add_kernel(keep_ref, other_ref, out_ref):
    for slot in range(8):
        total = keep_ref[slot].astype(jnp.float32) + other_ref[slot].astype(jnp.float32)
        out_ref[slot] = total.astype(out_ref.dtype)


def add_parts(keep, other):
    return pl.pallas_call(
        add_kernel,
        out_shape=jax.ShapeDtypeStruct(keep.shape, keep.dtype),
        in_specs=[VMEM] * 2,
        out_specs=VMEM,
    )(*on_chip(keep, other))


def keys_product(tok_ref, parts):
    groups, shards, piece, hd = parts[0][0].shape
    rows = groups * piece
    replica = lax.axis_index("replica")
    y_half_index = lax.axis_index("fsdp") % 2
    acc = jnp.zeros((tok_ref.shape[0], hd), jnp.float32)
    for f in range(shards):
        shard = (f % 8) * 2 + (y_half_index + f // 8) % 2
        for w_ref, flip_core, flip_plane in parts:
            half = (replica + flip_core) % 2
            quarter = (replica // 8 + flip_plane) % 2
            start = pl.multiple_of(((shard * 2 + half) * 2 + quarter) * rows, rows)
            acc = acc + jnp.dot(
                tok_ref[:, pl.ds(start, rows)],
                w_ref[:, f].reshape(rows, hd),
                preferred_element_type=jnp.float32,
            )
    return acc


def keys_near(tok_ref, near_ref, out_ref):
    out_ref[...] = keys_product(tok_ref, ((near_ref, 0, 0),))


def keys_mid(tok_ref, far_ref, near_other_ref, so_far_ref, out_ref):
    acc = keys_product(tok_ref, ((far_ref, 0, 1), (near_other_ref, 1, 0)))
    out_ref[...] = so_far_ref[...] + acc


def keys_last(tok_ref, far_other_ref, inv_ref, so_far_ref, out_ref):
    acc = so_far_ref[...] + keys_product(tok_ref, ((far_other_ref, 1, 1),))
    out_ref[...] = (acc * inv_ref[...]).astype(out_ref.dtype)


def step(
    tokens,
    norm_gain,
    key_weight,
    key_cotangent,
    outer_params,
    outer_momentum,
    inner_params,
    fragment,
    mix_step,
):
    rows, hd = key_weight.shape
    replica = lax.axis_index("replica")
    replicas = lax.axis_size("replica")
    core = replica % 2

    inv, keep, send = factor_parts(tokens, key_cotangent, rows)
    recv = permute(send, x_near)

    plane = replica // 8
    piece = rows // 16
    z_bits = (plane // 4, plane // 2 % 2, plane % 2)
    order = core * 8 + z_bits[2] * 4 + z_bits[1] * 2 + z_bits[0]
    gain_piece = lax.dynamic_slice_in_dim(norm_gain, order * piece, piece, 0).astype(jnp.float32)
    weight_piece = lax.dynamic_slice_in_dim(key_weight, order * piece, piece, 0).astype(jnp.float32)
    scaled_piece = (gain_piece[:, None] * weight_piece).astype(jnp.bfloat16)
    y_groups = [[2 * x + y for x in range(8)] for y in range(2)]
    w_row = lax.all_to_all(
        jnp.broadcast_to(scaled_piece[None], (8, piece, hd)),
        "fsdp",
        0,
        0,
        axis_index_groups=y_groups,
    )
    w_pieces = jnp.concatenate([w_row, permute(w_row, y_half)])[None]

    def doubled(values, move, bit):
        other = permute(values, move)
        return jnp.concatenate(
            [jnp.where(bit == 0, values, other), jnp.where(bit == 0, other, values)]
        )

    w_pieces = doubled(w_pieces, z_four, z_bits[0])
    w_near = doubled(w_pieces, z_two, z_bits[1])
    w_far = permute(w_near, z_one)
    w_near_other = permute(w_near, core_swap)
    w_far_other = permute(w_far, core_swap)
    part = add_parts(keep, recv)
    x_groups = [[4 * k + 2 * p + y for k in range(4) for y in range(2)] for p in range(2)]
    mine = lax.all_to_all(part, "fsdp", 0, 0, axis_index_groups=x_groups)

    blocks = (replicas // 2, 2, outer_params.shape[2] // replicas)

    def row_of(values):
        return lax.dynamic_index_in_dim(values, fragment, 0, keepdims=False).reshape(blocks)

    def half_of(values):
        return lax.dynamic_index_in_dim(values, core, 1, keepdims=False)

    inner_row = row_of(inner_params[0])
    halves = jnp.broadcast_to(
        inner_row.transpose(1, 0, 2)[None], (replicas // 2, 2, blocks[0], blocks[2])
    ).reshape(replicas, blocks[0], blocks[2])
    inner_all = lax.all_to_all(halves, "replica", 0, 0)
    total = jnp.sum(inner_all.astype(jnp.float32), axis=0)
    outer_now = half_of(row_of(outer_params))
    momentum_now = half_of(row_of(outer_momentum))
    pseudo_grad = outer_now - total / replicas
    momentum_next = 0.9 * momentum_now + pseudo_grad
    outer_next = outer_now - 0.7 * (pseudo_grad + 0.9 * momentum_next)
    own_outer = lax.dynamic_slice_in_dim(outer_next, replica // 2, 1, 0)
    own_momentum = lax.dynamic_slice_in_dim(momentum_next, replica // 2, 1, 0)
    outer_other = permute(outer_next, core_swap)
    outer_pair = jnp.where(
        core == 0,
        jnp.stack([outer_next, outer_other], axis=1),
        jnp.stack([outer_other, outer_next], axis=1),
    )
    mix_alpha = (mix_step[0].astype(jnp.float32) + 1.0) / (MIXSTEPS + 1.0)
    new_inner = mix_alpha * outer_pair + (1.0 - mix_alpha) * inner_row.astype(jnp.float32)
    new_inner = new_inner.astype(jnp.bfloat16).reshape(1, -1)

    out = jax.ShapeDtypeStruct((tokens.shape[0], hd), jnp.bfloat16)
    so_far = pltpu.VMEM(out.shape, jnp.float32)

    def keys(kernel, shape, *values):
        return pl.pallas_call(
            kernel, out_shape=shape, in_specs=[VMEM] * (1 + len(values)), out_specs=VMEM
        )(tokens, *on_chip(*values))

    part_keys = keys(keys_near, so_far, w_near)
    part_keys = keys(keys_mid, so_far, w_far, w_near_other, part_keys)
    key_out = keys(keys_last, out, w_far_other, inv, part_keys)

    factor = jnp.sum(mine.astype(jnp.float32), axis=0).T
    weight_grad = norm_gain.astype(jnp.float32)[:, None] * factor
    gain_grad = jnp.sum(key_weight.astype(jnp.float32) * factor, axis=1)
    return (key_out, weight_grad[None], gain_grad[None], own_outer, own_momentum, new_inner[None])


def solution(mesh):
    in_specs = (
        P(("replica", "fsdp"), None),
        P("fsdp"),
        P("fsdp", None),
        P(("replica", "fsdp"), None),
        P(None, "fsdp", None),
        P(None, "fsdp", None),
        P("replica", None, "fsdp", None),
        P(),
        P("replica"),
    )
    out_specs = (
        P(("replica", "fsdp"), None),
        P("replica", "fsdp", None),
        P("replica", "fsdp"),
        P("fsdp", "replica"),
        P("fsdp", "replica"),
        P("replica", "fsdp", None),
    )
    return jax.shard_map(step, mesh=mesh, in_specs=in_specs, out_specs=out_specs, check_vma=False)
```
